32 devices in a mesh: ctx: 8 (over y, x, core), tp: 4 (over z).
Axes of the slice: x: 2, y: 2, z: 4, core: 2. Of those that a mesh axis runs over, the one named last changes fastest.
Arguments:
- queries: bfloat16 [4096, 64, 128], P('ctx', 'tp'), may hold values from -5 to 5
- own_keys: bfloat16 [4096, 8, 128], P('ctx', 'tp'), may hold values from -5 to 5
- own_values: bfloat16 [4096, 8, 128], P('ctx', 'tp'), may hold values from -5 to 5
- cache_keys: bfloat16 [8, 32768, 128], P('tp', 'ctx'), may hold values from -5 to 5
- cache_values: bfloat16 [8, 32768, 128], P('tp', 'ctx'), may hold values from -5 to 5
- selected: int32 [8, 8, 8], P('ctx', 'tp'), may hold values from 0 to 63, as said below
- out_weight: bfloat16 [8192, 8192], P('tp'), may hold values from -0.0625 to 0.0625
Outputs:
- mixed: bfloat16 [4096, 8192], P('ctx', 'tp')
The draws below stay inside these ranges and needn't reach their ends.
Inputs may be any that keep to these rules, and one draw needn't show every extreme that they name: `selected`: for each query block and key head, 8 different cache blocks, each lying in the cache of a different index of ctx (blocks k * 8 to (k + 1) * 8 - 1 for index k), so that at most 1 of them lie in one index.
All inputs are finite; a program needn't handle non-finite values.
Results may differ from the reference program's by a relative error of at most 0.017.
Values may be sent and summed in bfloat16 or wider, within the bound.
A program may use at most 192 MiB of HBM per device.

```python
import jax
import jax.numpy as jnp
from jax import lax

D = 8192
HEADS = 64
KVH = 8
HD = 128
BLOCK = 512
TOPK = 8
CACHE_DEV = 4096
TOKENS = 4096
CACHE = 32768
N_TP = 4


def draw_queries(key, part):
    inner_key = jax.random.fold_in(key, 5)
    values_drawn = jnp.clip(jax.random.normal(inner_key, (TOKENS, HEADS, HD), jnp.float32), -5.0, 5.0)
    return values_drawn.astype(jnp.bfloat16)


def draw_own_keys(key, part):
    inner_key = jax.random.fold_in(key, 9)
    values_drawn = jnp.clip(jax.random.normal(inner_key, (TOKENS, KVH, HD), jnp.float32), -5.0, 5.0)
    return values_drawn.astype(jnp.bfloat16)


def draw_selected(key, part):
    row_count = TOKENS // BLOCK * KVH
    blocks_dev = CACHE_DEV // BLOCK
    owner_count = CACHE // CACHE_DEV
    row_keys = jax.random.split(jax.random.fold_in(key, 11), row_count)
    permuted = jax.vmap(lambda row_key: jax.random.permutation(row_key, owner_count))(row_keys)
    owner_of = permuted[:, :TOPK]
    inside = jax.random.randint(jax.random.fold_in(key, 13), (row_count, TOPK), 0, blocks_dev)
    chosen = owner_of * blocks_dev + inside
    return chosen.reshape(TOKENS // BLOCK, KVH, TOPK).astype(jnp.int32)


def level_of(key, dims, pieces, least, high):
    gain = 1.0
    for dim, parts in pieces:
        draws = jax.random.uniform(jax.random.fold_in(jax.random.fold_in(key, 6), dim), (parts,), jnp.float32, least / len(pieces), high / len(pieces))
        gain = gain * jnp.repeat(jnp.exp(draws), dims[dim] // parts).reshape((-1,) + (1,) * (len(dims) - 1 - dim))
    return gain


def noise(stream_key, dims, deviation, bound, cuts=(), held_as=jnp.bfloat16):
    factor_of = level_of(stream_key, dims, cuts, -0.22, 0.18) if cuts else 1.0
    entries = jax.random.normal(stream_key, dims, jnp.float32) * deviation * factor_of
    return jnp.minimum(jnp.maximum(entries, -bound), bound).astype(held_as)


def setup_inputs(seed: int = 0) -> dict:
    key_of = jax.random.split(jax.random.key(seed), 8)
    return {
        "queries": draw_queries(jax.random.fold_in(key_of[7], 71), 0),
        "own_keys": draw_own_keys(jax.random.fold_in(key_of[7], 71), 0),
        "own_values": noise(key_of[2], (TOKENS, KVH, HD), 1.0, 5.0, ((0, 8), (1, 4))),
        "cache_keys": noise(key_of[3], (KVH, CACHE, HD), 1.0, 5.0, ((0, 4), (1, 8))),
        "cache_values": noise(key_of[4], (KVH, CACHE, HD), 1.0, 5.0, ((0, 4), (1, 8))),
        "selected": draw_selected(jax.random.fold_in(key_of[7], 71), 0),
        "out_weight": noise(key_of[6], (D, D), D ** -0.5, 0.0625, ((0, 4),)),
    }


def attend(query_block, key_set, value_set):
    rows_count = query_block.shape[0]
    total_keys = key_set.shape[0]
    remote_count = total_keys - rows_count
    scores = jnp.einsum("tgd,kd->gtk", query_block.astype(jnp.float32), key_set.astype(jnp.float32))
    scores = scores * (query_block.shape[2] ** -0.5)
    column = lax.broadcasted_iota(jnp.int32, (rows_count, total_keys), 1)
    row_index = lax.broadcasted_iota(jnp.int32, (rows_count, total_keys), 0)
    allowed = (column < remote_count) | (column - remote_count <= row_index)
    scores = jnp.where(allowed[None], scores, -jnp.inf)
    largest = jnp.max(scores, axis=2, keepdims=True)
    powers = jnp.exp(scores - largest)
    weights = (powers / jnp.sum(powers, axis=2, keepdims=True)).astype(jnp.bfloat16)
    mixed_heads = jnp.einsum("gtk,kd->tgd", weights.astype(jnp.float32), value_set.astype(jnp.float32))
    return mixed_heads.astype(jnp.bfloat16)


def reference(queries, own_keys, own_values, cache_keys, cache_values, selected, out_weight):
    group_size = HEADS // KVH
    block_count = CACHE // BLOCK
    key_table = cache_keys.reshape(KVH, block_count, BLOCK, HD)
    value_table = cache_values.reshape(KVH, block_count, BLOCK, HD)

    def one_block(block_index):
        start = block_index * BLOCK
        query_block = lax.dynamic_slice_in_dim(queries, start, BLOCK, 0)
        block_keys = lax.dynamic_slice_in_dim(own_keys, start, BLOCK, 0)
        block_values = lax.dynamic_slice_in_dim(own_values, start, BLOCK, 0)
        chosen_all = selected[block_index]
        outputs = []
        for kv_head in range(KVH):
            chosen_ids = chosen_all[kv_head]
            key_set = jnp.concatenate([key_table[kv_head][chosen_ids].reshape(TOPK * BLOCK, HD), block_keys[:, kv_head]], axis=0)
            value_set = jnp.concatenate([value_table[kv_head][chosen_ids].reshape(TOPK * BLOCK, HD), block_values[:, kv_head]], axis=0)
            outputs.append(attend(query_block[:, kv_head * group_size:(kv_head + 1) * group_size], key_set, value_set))
        return jnp.concatenate(outputs, axis=1)

    attended = lax.map(one_block, jnp.arange(TOKENS // BLOCK, dtype=jnp.int32))
    attended = attended.reshape(TOKENS, D)
    share_rows = D // N_TP
    total_sum = jnp.zeros((TOKENS, D), jnp.float32)
    for group_index in range(N_TP):
        partial_value = jnp.dot(attended[:, group_index * share_rows:(group_index + 1) * share_rows], out_weight[group_index * share_rows:(group_index + 1) * share_rows], preferred_element_type=jnp.float32).astype(jnp.bfloat16)
        partial_value = lax.optimization_barrier(partial_value)
        total_sum = total_sum + partial_value.astype(jnp.float32)
    return total_sum.astype(jnp.bfloat16)
```

```python
import functools

import jax
import jax.numpy as jnp
from jax import lax
from jax.experimental import pallas as pl
from jax.experimental.pallas import tpu as pltpu
from jax.sharding import PartitionSpec as P

LOG2E = 1.4426950408889634


def attention_kernel(start, group, owner_ref, query_ref, own_keys, own_values, got, out_ref,
                     keys, values, scores_a, scores_b, peaks, powers_a, powers_b, total, sems):
    rows, width = query_ref.shape
    head_width = own_keys.shape[-1]
    kv_local = own_keys.shape[0]
    picked = owner_ref.shape[1]
    block = got.shape[3]
    stop = start + rows
    cached = picked * block
    units = width // head_width
    factor = head_width ** -0.5 * LOG2E

    copies = []
    for head in range(kv_local):
        for slot in range(picked):
            place = pl.ds(slot * block, block)
            owner = owner_ref[head, slot]
            copies.append(pltpu.make_async_copy(got.at[owner, head, 0], keys.at[head, place], sems.at[len(copies)]))
            copies.append(pltpu.make_async_copy(
                got.at[owner, head, 1], values.at[head, place, pl.ds(0, head_width)], sems.at[len(copies)]))
        place = pl.ds(cached, stop)
        copies.append(pltpu.make_async_copy(own_keys.at[head, pl.ds(0, stop)], keys.at[head, place], sems.at[len(copies)]))
        copies.append(pltpu.make_async_copy(
            own_values.at[head, pl.ds(0, stop)], values.at[head, place, pl.ds(0, head_width)], sems.at[len(copies)]))
    for copy in copies:
        copy.start()
    for head in range(kv_local):
        values[head, :, head_width:] = jnp.ones((cached + stop, head_width), jnp.bfloat16)
    for copy in copies:
        copy.wait()

    step = 2 * block
    cuts = [(first, min(step, cached - first)) for first in range(0, cached, step)] + [(cached, stop)]

    def phase(unit, scores_now, scores_next, powers_now, powers_before, stages=(True, True, True)):
        ahead, middle, last = stages
        following = unit + 1
        before = unit - 1
        if ahead:
            query = query_ref[:, pl.ds(pl.multiple_of(following * head_width, head_width), head_width)]
            next_head = following // group
        if middle:
            peak = peaks[...]
        if last:
            before_head = before // group
        lanes = None
        for index, (first, size) in enumerate(cuts):
            if ahead:
                part = lax.dot_general(query, keys[next_head, first:first + size], (((1,), (1,)), ((), ())),
                                       preferred_element_type=jnp.float32)
                if first == cached:
                    row = lax.broadcasted_iota(jnp.int32, part.shape, 0)
                    column = lax.broadcasted_iota(jnp.int32, part.shape, 1)
                    part = jnp.where(column <= row + start, part, -jnp.inf)
                scores_next[:, first:first + size] = part
                for lane in range(0, size, head_width):
                    piece = part[:, lane:lane + head_width]
                    lanes = piece if lanes is None else jnp.maximum(lanes, piece)
            if middle:
                for lane in range(first, first + size, head_width):
                    powers_now[:, lane:lane + head_width] = jnp.exp2(
                        (scores_now[:, lane:lane + head_width] - peak) * factor).astype(jnp.bfloat16)
            if last:
                term = jnp.dot(powers_before[:, first:first + size], values[before_head, first:first + size],
                               preferred_element_type=jnp.float32)
                if index == 0:
                    total[...] = term
                elif index < len(cuts) - 1:
                    total[...] += term
                else:
                    term = total[...] + term
                    out_ref[:, pl.ds(pl.multiple_of(before * head_width, head_width), head_width)] = (
                        term[:, :head_width] / term[:, head_width:]).astype(jnp.bfloat16)
        if ahead:
            peaks[...] = jnp.broadcast_to(jnp.max(lanes, axis=1, keepdims=True), peaks.shape)

    phase(-1, scores_a, scores_b, powers_a, powers_b, (True, False, False))
    phase(0, scores_b, scores_a, powers_b, powers_a, (True, True, False))

    def pair(index, carry):
        phase(2 * index + 1, scores_a, scores_b, powers_a, powers_b)
        phase(2 * index + 2, scores_b, scores_a, powers_b, powers_a)
        return carry

    lax.fori_loop(0, units // 2 - 1, pair, 0)
    phase(units - 1, scores_a, scores_b, powers_a, powers_b, (False, True, True))
    phase(units, scores_b, scores_a, powers_b, powers_a, (False, False, True))


def attend(start, group, owners, query, own_keys, own_values, got):
    rows = query.shape[0]
    head_width = own_keys.shape[-1]
    kv_local = own_keys.shape[0]
    picked = owners.shape[1]
    block = got.shape[3]
    count = picked * block + start + rows
    full = pl.BlockSpec(memory_space=pltpu.VMEM)
    any_place = pl.BlockSpec(memory_space=pl.ANY)
    units = query.shape[1] // head_width
    return pl.pallas_call(
        functools.partial(attention_kernel, start, group),
        out_shape=jax.ShapeDtypeStruct(query.shape, jnp.bfloat16),
        in_specs=[pl.BlockSpec(memory_space=pltpu.SMEM), full, any_place, any_place, any_place],
        out_specs=full,
        scratch_shapes=[
            pltpu.VMEM((kv_local, count, head_width), jnp.bfloat16),
            pltpu.VMEM((kv_local, count, 2 * head_width), jnp.bfloat16),
            pltpu.VMEM((rows, count), jnp.float32),
            pltpu.VMEM((rows, count), jnp.float32),
            pltpu.VMEM((rows, head_width), jnp.float32),
            pltpu.VMEM((rows, count), jnp.bfloat16),
            pltpu.VMEM((rows, count), jnp.bfloat16),
            pltpu.VMEM((rows, 2 * head_width), jnp.float32),
            pltpu.SemaphoreType.DMA((kv_local * 2 * (picked + 1),)),
        ],
        compiler_params=pltpu.CompilerParams(vmem_limit_bytes=48 * 1024 * 1024),
        cost_estimate=pl.CostEstimate(
            flops=8 * rows * count * head_width * units, transcendentals=rows * count * units,
            bytes_accessed=4 * kv_local * count * head_width),
        name=f"attend_{start}",
    )(owners, query, own_keys, own_values, got)


CHUNKS = 2


def shards(queries, own_keys, own_values, cache_keys, cache_values, selected, out_weight):
    block_rows = queries.shape[0]
    kv_local, _, head_width = cache_keys.shape
    blocks_dev = cache_keys.shape[1] // block_rows
    group = queries.shape[1] // kv_local
    picked = selected[0]
    owners = picked // blocks_dev
    owner_count = lax.axis_size("ctx")
    match = owners[:, :, None] == jnp.arange(owner_count, dtype=jnp.int32)[None, None, :]
    request = jnp.sum(jnp.where(match, (picked % blocks_dev)[:, :, None], 0), axis=1).T
    wanted = lax.all_to_all(request, "ctx", split_axis=0, concat_axis=0, tiled=True)
    heads = jnp.arange(kv_local, dtype=jnp.int32)[None, :]
    shape = (kv_local, blocks_dev, block_rows, head_width)
    sent = jnp.stack([cache_keys.reshape(shape)[heads, wanted], cache_values.reshape(shape)[heads, wanted]], axis=2)
    got = lax.all_to_all(sent, "ctx", split_axis=0, concat_axis=0, tiled=True)
    query = queries.reshape(block_rows, -1)
    keys = jnp.transpose(own_keys, (1, 0, 2))
    values = jnp.transpose(own_values, (1, 0, 2))
    rows = block_rows // CHUNKS
    outputs = []
    for start in range(0, block_rows, rows):
        attended = attend(start, group, owners, query[start:start + rows], keys, values, got)
        term = jnp.dot(attended, out_weight, preferred_element_type=jnp.float32).astype(jnp.bfloat16)
        outputs.append(lax.psum_scatter(term, "tp", scatter_dimension=1, tiled=True))
    return jnp.concatenate(outputs, axis=0)


def solution(mesh):
    in_specs = (
        P("ctx", "tp", None),
        P("ctx", "tp", None),
        P("ctx", "tp", None),
        P("tp", "ctx", None),
        P("tp", "ctx", None),
        P("ctx", "tp", None),
        P("tp", None),
    )
    return jax.shard_map(shards, mesh=mesh, in_specs=in_specs, out_specs=P("ctx", "tp"), check_vma=False)
```

```python
import functools

import jax
import jax.numpy as jnp
from jax import lax
from jax.experimental import pallas as pl
from jax.experimental.pallas import tpu as pltpu
from jax.sharding import PartitionSpec as P

LOG2E = 1.4426950408889634


def gather_kernel(wanted_ref, keys_ref, values_ref, out_ref):
    out_ref[0, 0] = keys_ref[0]
    out_ref[0, 1] = values_ref[0]


def gather(head, wanted, cache_keys, cache_values, block):
    count = wanted.shape[0]
    head_width = cache_keys.shape[2]
    spec = pl.BlockSpec((1, block, head_width), lambda owner, ids: (head, ids[owner, head], 0))
    return pl.pallas_call(
        gather_kernel,
        out_shape=jax.ShapeDtypeStruct((count, 2, block, head_width), cache_keys.dtype),
        grid_spec=pltpu.PrefetchScalarGridSpec(
            num_scalar_prefetch=1, grid=(count,), in_specs=[spec, spec],
            out_specs=pl.BlockSpec((1, 2, block, head_width), lambda owner, ids: (owner, 0, 0, 0))),
        compiler_params=pltpu.CompilerParams(vmem_limit_bytes=60 * 1024 * 1024),
        name=f"gather_{head}",
    )(wanted, cache_keys, cache_values)


def fused_kernel(start, rows, tile, owner_ref, query_ref, own_keys, own_values, got, earlier, weight, term_ref,
                 held, mine, weight_sem, *scratch):
    copy = pltpu.make_async_copy(weight, held, weight_sem)
    attention_kernel(start, rows, owner_ref, query_ref, own_keys, own_values, got, mine, *scratch, copy=copy)
    copy.wait()
    depth = earlier.shape[1]

    def column(index, carry):
        place = pl.ds(pl.multiple_of(index * tile, tile), tile)
        term = jnp.dot(mine[...], held[depth:, place], preferred_element_type=jnp.float32)
        if depth:
            term += jnp.dot(earlier[...], held[:depth, place], preferred_element_type=jnp.float32)
        term_ref[:, place] = term.astype(term_ref.dtype)
        return carry

    lax.fori_loop(0, weight.shape[1] // tile, column, 0)


def attention_kernel(start, rows, owner_ref, query_ref, own_keys, own_values, got, out_ref,
                     keys, values, scores_a, scores_b, peaks, powers_a, powers_b, total, sems, copy=None):
    all_rows, width = query_ref.shape
    head_width = own_keys.shape[-1]
    picked = owner_ref.shape[0]
    block = got.shape[2]
    stop = start + all_rows
    cached = picked * block
    group = width // head_width
    units = group * (all_rows // rows)
    factor = head_width ** -0.5 * LOG2E

    copies = []
    for slot in range(picked):
        place = pl.ds(slot * block, block)
        owner = owner_ref[slot]
        copies.append(pltpu.make_async_copy(got.at[owner, 0], keys.at[place], sems.at[len(copies)]))
        copies.append(pltpu.make_async_copy(
            got.at[owner, 1], values.at[place, pl.ds(0, head_width)], sems.at[len(copies)]))
    place = pl.ds(cached, stop)
    copies.append(pltpu.make_async_copy(own_keys.at[pl.ds(0, stop)], keys.at[place], sems.at[len(copies)]))
    copies.append(pltpu.make_async_copy(
        own_values.at[pl.ds(0, stop)], values.at[place, pl.ds(0, head_width)], sems.at[len(copies)]))
    for item in copies:
        item.start()
    values[:, head_width:] = jnp.ones((cached + stop, head_width), jnp.bfloat16)
    for item in copies:
        item.wait()
    if copy is not None:
        copy.start()

    step = 2 * block
    cuts = [(first, min(step, cached - first)) for first in range(0, cached, step)] + [(cached, stop)]

    def place_of(unit):
        row = pl.multiple_of(unit // group * rows, rows)
        return row, (pl.ds(row, rows), pl.ds(pl.multiple_of(unit % group * head_width, head_width), head_width))

    def phase(unit, scores_now, scores_next, powers_now, powers_before, stages=(True, True, True)):
        ahead, middle, last = stages
        if ahead:
            first_row, place = place_of(unit + 1)
            query = query_ref[place]
        if middle:
            peak = peaks[...]
        lanes = None
        for index, (first, size) in enumerate(cuts):
            if ahead:
                part = lax.dot_general(query, keys[first:first + size], (((1,), (1,)), ((), ())),
                                       preferred_element_type=jnp.float32)
                if first == cached:
                    row = lax.broadcasted_iota(jnp.int32, part.shape, 0)
                    column = lax.broadcasted_iota(jnp.int32, part.shape, 1)
                    part = jnp.where(column <= row + (first_row + start), part, -jnp.inf)
                scores_next[:, first:first + size] = part
                for lane in range(0, size, head_width):
                    piece = part[:, lane:lane + head_width]
                    lanes = piece if lanes is None else jnp.maximum(lanes, piece)
            if middle:
                for lane in range(first, first + size, head_width):
                    powers_now[:, lane:lane + head_width] = jnp.exp2(
                        (scores_now[:, lane:lane + head_width] - peak) * factor).astype(jnp.bfloat16)
            if last:
                term = jnp.dot(powers_before[:, first:first + size], values[first:first + size],
                               preferred_element_type=jnp.float32)
                if index == 0:
                    total[...] = term
                elif index < len(cuts) - 1:
                    total[...] += term
                else:
                    term = total[...] + term
                    out_ref[place_of(unit - 1)[1]] = (
                        term[:, :head_width] / term[:, head_width:]).astype(jnp.bfloat16)
        if ahead:
            peaks[...] = jnp.broadcast_to(jnp.max(lanes, axis=1, keepdims=True), peaks.shape)

    phase(-1, scores_a, scores_b, powers_a, powers_b, (True, False, False))
    phase(0, scores_b, scores_a, powers_b, powers_a, (True, True, False))

    def pair(index, carry):
        phase(2 * index + 1, scores_a, scores_b, powers_a, powers_b)
        phase(2 * index + 2, scores_b, scores_a, powers_b, powers_a)
        return carry

    lax.fori_loop(0, units // 2 - 1, pair, 0)
    phase(units - 1, scores_a, scores_b, powers_a, powers_b, (False, True, True))
    phase(units, scores_b, scores_a, powers_b, powers_a, (False, False, True))


def attend(name, start, rows, owners, query, own_keys, own_values, got, earlier=None, weight=None):
    all_rows, width = query.shape
    head_width = own_keys.shape[-1]
    picked = owners.shape[0]
    count = picked * got.shape[2] + start + all_rows
    full = pl.BlockSpec(memory_space=pltpu.VMEM)
    any_place = pl.BlockSpec(memory_space=pl.ANY)
    heads = width // head_width
    scratch = [
        pltpu.VMEM((count, head_width), jnp.bfloat16),
        pltpu.VMEM((count, 2 * head_width), jnp.bfloat16),
        pltpu.VMEM((rows, count), jnp.float32),
        pltpu.VMEM((rows, count), jnp.float32),
        pltpu.VMEM((rows, head_width), jnp.float32),
        pltpu.VMEM((rows, count), jnp.bfloat16),
        pltpu.VMEM((rows, count), jnp.bfloat16),
        pltpu.VMEM((rows, 2 * head_width), jnp.float32),
        pltpu.SemaphoreType.DMA((2 * (picked + 1),)),
    ]
    specs = [pl.BlockSpec(memory_space=pltpu.SMEM), full, any_place, any_place, any_place]
    operands = [owners, query, own_keys, own_values, got]
    flops = 8 * all_rows * count * head_width * heads
    moved = 4 * count * head_width
    limit = 40
    if weight is None:
        kernel = functools.partial(attention_kernel, start, rows)
        shape = query.shape
    else:
        kernel = functools.partial(fused_kernel, start, rows, 512)
        shape = (all_rows, weight.shape[1])
        scratch = [pltpu.VMEM(weight.shape, weight.dtype), pltpu.VMEM(query.shape, jnp.bfloat16),
                   pltpu.SemaphoreType.DMA] + scratch
        specs = specs + [full, any_place]
        operands = operands + [earlier, weight]
        flops += 2 * all_rows * weight.shape[0] * weight.shape[1]
        moved += 2 * weight.shape[0] * weight.shape[1]
        limit = 60
    return pl.pallas_call(
        kernel,
        out_shape=jax.ShapeDtypeStruct(shape, jnp.bfloat16),
        in_specs=specs,
        out_specs=full,
        scratch_shapes=scratch,
        compiler_params=pltpu.CompilerParams(vmem_limit_bytes=limit * 1024 * 1024),
        cost_estimate=pl.CostEstimate(
            flops=flops, transcendentals=all_rows * count * heads, bytes_accessed=moved),
        name=name,
    )(*operands)


def shards(queries, own_keys, own_values, cache_keys, cache_values, selected, out_weight):
    block_rows = queries.shape[0]
    kv_local, _, head_width = cache_keys.shape
    blocks_dev = cache_keys.shape[1] // block_rows
    group_width = queries.shape[1] // kv_local * head_width
    picked = selected[0]
    owners = picked // blocks_dev
    owner_count = lax.axis_size("ctx")
    match = owners[:, :, None] == jnp.arange(owner_count, dtype=jnp.int32)[None, None, :]
    request = jnp.sum(jnp.where(match, (picked % blocks_dev)[:, :, None], 0), axis=1).T
    wanted = lax.all_to_all(request, "ctx", split_axis=0, concat_axis=0, tiled=True)
    got = []
    for head in range(kv_local):
        sent = gather(head, wanted, cache_keys, cache_values, block_rows)
        if got:
            sent, got[-1] = lax.optimization_barrier((sent, got[-1]))
        got.append(lax.all_to_all(sent, "ctx", split_axis=0, concat_axis=0, tiled=True))
    query = queries.reshape(block_rows, -1)
    keys = jnp.transpose(own_keys, (1, 0, 2))
    values = jnp.transpose(own_values, (1, 0, 2))

    def part(head, start, stop, rows, *more):
        return attend(f"attend_{head}_{start}", start, rows, owners[head],
                      query[start:stop, head * group_width:(head + 1) * group_width],
                      keys[head], values[head], got[head], *more)

    last = kv_local - 1
    short = block_rows // 4
    rest = (block_rows - short) // 2
    most = block_rows - short
    if last:
        first = [part(head, 0, most, rest) for head in range(last)]
        term = part(last, 0, short, short, jnp.concatenate([item[:short] for item in first], axis=1), out_weight)
        term, query = lax.optimization_barrier((term, query))
        whole = [jnp.concatenate([first[head][short:], part(head, most, block_rows, short)], axis=0)
                 for head in range(last)]
    else:
        attended = part(last, 0, short, short)
        term = jnp.dot(attended, out_weight, preferred_element_type=jnp.float32).astype(jnp.bfloat16)
        term, query = lax.optimization_barrier((term, query))
        whole = []
    outputs = [lax.psum_scatter(term, "tp", scatter_dimension=1, tiled=True)]
    attended = jnp.concatenate(whole + [part(last, short, block_rows, rest)], axis=1)
    term = jnp.dot(attended, out_weight, preferred_element_type=jnp.float32).astype(jnp.bfloat16)
    outputs.append(lax.psum_scatter(term, "tp", scatter_dimension=1, tiled=True))
    return jnp.concatenate(outputs, axis=0)


def solution(mesh):
    in_specs = (
        P("ctx", "tp", None),
        P("ctx", "tp", None),
        P("ctx", "tp", None),
        P("tp", "ctx", None),
        P("tp", "ctx", None),
        P("ctx", "tp", None),
        P("tp", None),
    )
    return jax.shard_map(shards, mesh=mesh, in_specs=in_specs, out_specs=P("ctx", "tp"), check_vma=False)
```
